256 devices in a mesh: dp: 4 (over x), ep: 64 (over y, z, core).
Axes of the slice: x: 4, y: 4, z: 8, core: 2. Of those that a mesh axis runs over, the one named last changes fastest.
Arguments:
- tokens: bfloat16 [32768, 2048], P(('dp', 'ep'))
- cotangent: bfloat16 [32768, 2048], P(('dp', 'ep'))
- expert_ids: int32 [32768, 8], P(('dp', 'ep')), may hold values from 0 to 63, all different within a row; in each aligned block of 128 rows (0 to 127, 128 to 255, ...) at most 18 rows name the same one
- route_weights: bfloat16 [32768, 8], P(('dp', 'ep')), may hold values from 0.029907227 to 0.3984375
- weights: bfloat16 [64, 3, 2048, 384], P('ep')
- first_moment: bfloat16 [64, 3, 2048, 384], P('ep', None, 'dp'), may hold values from -4 to 4
- second_moment: bfloat16 [64, 3, 2048, 384], P('ep', None, 'dp'), may hold values from 0.049804688 to 0.5
Outputs:
- token_grad: bfloat16 [32768, 2048], P(('dp', 'ep'))
- routing_grad: bfloat16 [32768, 8], P(('dp', 'ep'))
- new_first: bfloat16 [64, 3, 2048, 384], P('ep', None, 'dp')
- new_second: bfloat16 [64, 3, 2048, 384], P('ep', None, 'dp')
- update: bfloat16 [64, 3, 2048, 384], P('ep', None, 'dp')
The draws below stay inside these ranges and needn't reach their ends.
Inputs may be any that keep to these rules, and one draw needn't show every extreme that they name: `expert_ids`: among the 128 rows of one device no expert is named by more than 18 rows.
All inputs are finite; a program needn't handle non-finite values.
Results may differ from the reference program's by a relative error of at most 0.0057.
Values may be sent and summed in bfloat16 or wider, within the bound.
No kernel may reach another device: no remote copies, remote signals or barrier semaphores. Data moves between devices by JAX's collectives and lax.ppermute only.
A program may use at most 128 MiB of HBM per device.

```python
import math
import jax
import jax.numpy as jnp
import numpy as np
from jax import lax

D = 2048
HID = 384
TOPK = 8
ADAM_STEP = 10
TOK_DEV = 128
EXPERTS = 64
CAP = 18
TOKENS = 32768


def draw_weights(key, part):
    key_base = jax.random.fold_in(key, 101)
    key_jitter = jax.random.fold_in(key, 202)
    expert = jnp.arange(EXPERTS, dtype=jnp.float32)
    ramp = 0.6 * 3.0 ** (expert / max(EXPERTS - 1, 1))
    jitter = jnp.exp(jax.random.uniform(key_jitter, (EXPERTS, 3), minval=-0.15, maxval=0.15))
    fanin = jnp.array([D ** (-0.5), D ** (-0.5), HID ** (-0.5)], jnp.float32)
    factor = ramp[:, None] * jitter * fanin[None, :]
    base = jnp.clip(jax.random.normal(key_base, (EXPERTS, 3, D, HID)), -4.0, 4.0)
    return (base * factor[:, :, None, None]).astype(jnp.bfloat16)


def rising_columns(key, salt):
    key_base = jax.random.fold_in(key, salt)
    key_jitter = jax.random.fold_in(key, salt + 7)
    key_sign = jax.random.fold_in(key, salt + 11)
    key_size = jax.random.fold_in(key, salt + 13)
    feature = jnp.arange(D, dtype=jnp.float32) / max(D - 1, 1)
    jitter = jnp.exp(jax.random.uniform(key_jitter, (D,), minval=-0.1, maxval=0.1))
    feature_sign = jax.random.rademacher(key_sign, (D,)).astype(jnp.float32)
    offset_size = jax.random.uniform(key_size, (D,), minval=0.5, maxval=1.5)
    column_scale = 0.6 * 3.0 ** feature * jitter
    base = jnp.clip(jax.random.normal(key_base, (TOKENS, D)), -4.0, 4.0)
    shared = 0.4 * offset_size * feature_sign
    return ((base + shared[None, :]) * column_scale[None, :]).astype(jnp.bfloat16)


def draw_tokens(key, part):
    return rising_columns(key, 303)


def draw_cotangent(key, part):
    return rising_columns(key, 404)


def shard_levels(key, dims, split, smallest, top_value):
    factor_of = 1.0
    for axis_at, parts in split:
        draws = jax.random.uniform(jax.random.fold_in(jax.random.fold_in(key, 6), axis_at), (parts,), jnp.float32, smallest / len(split), top_value / len(split))
        factor_of = factor_of * jnp.repeat(jnp.exp(draws), dims[axis_at] // parts).reshape((-1,) + (1,) * (len(dims) - 1 - axis_at))
    return factor_of


def routed_block(rng, own, number, rows, amount, top, limit, skew):
    ranking = jax.random.permutation(rng, amount)
    heavy_load, common = load_shares(amount, rows * top, limit, skew, True), load_shares(amount, rows * top, limit, skew, False)
    places = jnp.arange(amount)

    def named(tallies, turn):
        used = int((tallies > 0).sum())
        fixed = max(1, used // 4)
        moved = fixed + (places - fixed + turn * (used - fixed)) % max(1, amount - fixed)
        return jnp.zeros((amount,), jnp.int32).at[ranking[jnp.where(places < fixed, places, moved)]].set(jnp.asarray(tallies, jnp.int32))

    tallies = jnp.where(number % 4 == 0, named(heavy_load, number // 4), named(common, number - number // 4 - 1))
    mixed = jax.random.permutation(jax.random.fold_in(own, 3), amount)
    giver, taker = mixed[0:amount // 2 * 2:2], mixed[1:amount // 2 * 2:2]
    slack = jnp.minimum(tallies[giver] - 1, limit - tallies[taker]) // 2
    slack = jnp.where((giver == ranking[0]) | (taker == ranking[0]) | (tallies[taker] == 0), 0, jnp.maximum(slack, 0))
    moved = jax.random.randint(jax.random.fold_in(own, 4), (amount // 2,), 0, 1 << 20) % (slack + 1)
    tallies = tallies.at[giver].add(-moved).at[taker].add(moved)
    items = jnp.searchsorted(jnp.cumsum(tallies), jnp.arange(rows * top), side="right").astype(jnp.int32)
    listing = items.reshape(top, rows).T
    listing = listing[jax.random.permutation(jax.random.fold_in(own, 1), rows)]
    turn = jax.random.randint(jax.random.fold_in(own, 2), (rows, 1), 0, top)
    return jnp.take_along_axis(listing, (jnp.arange(top)[None, :] + turn) % top, axis=1)


def load_shares(amount, total, bound, skew, full):
    weights = [(1 << 20) // math.isqrt(rank ** skew) + 1 for rank in range(1, amount + 1)]
    largest = bound if full else min(bound, max(-(-total // amount), total * weights[0] // sum(weights)))
    least = 1 if total - largest >= amount - 1 else 0
    given, rest = [largest] + [least] * (amount - 1), total - largest - least * (amount - 1)
    while rest > 0:
        movable = [i for i in range(1, amount) if given[i] < largest] or [i for i in range(1, amount) if given[i] < bound]
        mass, budget = sum([weights[i] for i in movable]), rest
        for i in movable:
            more = min(bound - given[i], max(1, budget * weights[i] // mass), rest)
            given[i] = given[i] + more
            rest = rest - more
    return np.array(given)


def centred(own_key, shape, spread, bound, pieces=(), kind=jnp.bfloat16):
    factor_of = shard_levels(own_key, shape, pieces, -0.22, 0.18) if pieces else 1.0
    result = jax.random.normal(own_key, shape, jnp.float32) * spread * factor_of
    return jnp.minimum(jnp.maximum(result, -bound), bound).astype(kind)


def setup_inputs(seed: int = 0) -> dict:
    arg_keys = jax.random.split(jax.random.key(seed), 8)
    tokens = draw_tokens(jax.random.fold_in(arg_keys[7], 71), 0)
    cotangent = draw_cotangent(jax.random.fold_in(arg_keys[7], 71), 0)
    expert_ids_keys = jax.random.split(jax.random.fold_in(arg_keys[2], 1), TOKENS // TOK_DEV)
    expert_ids_turns = jax.random.permutation(jax.random.fold_in(arg_keys[2], 3), TOKENS // TOK_DEV)
    expert_ids = jax.vmap(lambda own, number: routed_block(jax.random.fold_in(arg_keys[2], 2), own, number, TOK_DEV, EXPERTS, TOPK, CAP, 1))(expert_ids_keys, expert_ids_turns).reshape((TOKENS, TOPK))
    route_weights = jnp.clip(jnp.exp(math.log(0.3984375) - 2.5894505 * jax.random.uniform(arg_keys[3], (TOKENS, TOPK), jnp.float32) ** shard_levels(arg_keys[3], (TOKENS, TOPK), ((0, 256),), -0.2, 0.2)), 0.029907227, 0.3984375).astype(jnp.bfloat16)
    weights = draw_weights(jax.random.fold_in(arg_keys[7], 71), 0)
    first_moment = centred(arg_keys[5], (EXPERTS, 3, D, HID), 0.3, 4.0, ((0, 64), (2, 4)))
    second_moment = jnp.clip(jnp.exp(math.log(0.5) - 2.306499 * jax.random.uniform(arg_keys[6], (EXPERTS, 3, D, HID), jnp.float32) ** shard_levels(arg_keys[6], (EXPERTS, 3, D, HID), ((0, 64), (2, 4)), -0.2, 0.2)), 0.049804688, 0.5).astype(jnp.bfloat16)
    return {"tokens": tokens, "cotangent": cotangent, "expert_ids": expert_ids, "route_weights": route_weights, "weights": weights, "first_moment": first_moment, "second_moment": second_moment}


def reference(tokens, cotangent, expert_ids, route_weights, weights, first_moment, second_moment):
    blocks_count = TOKENS // TOK_DEV
    pairs = TOK_DEV * TOPK
    sentinel = blocks_count * pairs
    ids_blocks = expert_ids.reshape(blocks_count, pairs)
    onehot = (ids_blocks[:, :, None] == jnp.arange(EXPERTS, dtype=jnp.int32)[None, None, :]).astype(jnp.int32)
    position = (lax.optimization_barrier(jnp.sum(jnp.cumsum(onehot, 1) * onehot, 2)) - 1).astype(jnp.int32)
    block_index = jnp.broadcast_to(jnp.arange(blocks_count, dtype=jnp.int32)[:, None], (blocks_count, pairs))
    flat_index = jnp.arange(sentinel, dtype=jnp.int32).reshape(blocks_count, pairs)
    table = jnp.full((EXPERTS, blocks_count, CAP), sentinel, jnp.int32).at[ids_blocks, block_index, position].set(flat_index)
    weight_flat = route_weights.reshape(-1)

    def per_expert(carry, inputs):
        expert_weights, expert_table = inputs
        slot_index = expert_table.reshape(-1)
        valid = slot_index < sentinel
        safe_index = jnp.where(valid, slot_index, 0).astype(jnp.int32)
        token_row = (safe_index // TOPK).astype(jnp.int32)
        rows_x = jnp.where(valid[:, None], tokens[token_row], jnp.zeros((), tokens.dtype))
        rows_cot = jnp.where(valid[:, None], cotangent[token_row], jnp.zeros((), cotangent.dtype))
        rows_weight = jnp.where(valid, weight_flat[safe_index].astype(jnp.float32), jnp.float32(0.0))
        w_gate = expert_weights[0]
        w_up = expert_weights[1]
        w_down = expert_weights[2]
        gate_val = jnp.dot(rows_x, w_gate, preferred_element_type=jnp.float32)
        up_val = jnp.dot(rows_x, w_up, preferred_element_type=jnp.float32)
        sigmoid_gate = jax.nn.sigmoid(gate_val)
        activated = gate_val * sigmoid_gate
        hidden = lax.optimization_barrier((activated * up_val).astype(jnp.bfloat16))
        back_val = jnp.dot(rows_cot, w_down, preferred_element_type=jnp.float32)
        route_part = lax.optimization_barrier(lax.optimization_barrier(jnp.sum(hidden.astype(jnp.float32) * back_val, 1)).astype(jnp.bfloat16))
        scaled = rows_weight[:, None] * back_val
        dgate = (scaled * up_val * sigmoid_gate * (1.0 + gate_val * (1.0 - sigmoid_gate))).astype(jnp.bfloat16)
        dup = (scaled * activated).astype(jnp.bfloat16)
        down_cot = (rows_weight[:, None] * rows_cot.astype(jnp.float32)).astype(jnp.bfloat16)
        slot_back = jnp.dot(dgate, w_gate.T, preferred_element_type=jnp.float32) + jnp.dot(dup, w_up.T, preferred_element_type=jnp.float32)
        slot_back = lax.optimization_barrier(slot_back.astype(jnp.bfloat16))
        grad_gate = jnp.dot(rows_x.T, dgate, preferred_element_type=jnp.float32)
        grad_up = jnp.dot(rows_x.T, dup, preferred_element_type=jnp.float32)
        grad_down = jnp.dot(down_cot.T, hidden, preferred_element_type=jnp.float32)
        token_acc = carry[0].at[jnp.where(valid, token_row, TOKENS).astype(jnp.int32)].add(slot_back.astype(jnp.float32), mode='drop')
        route_acc = carry[1].at[jnp.where(valid, slot_index, sentinel).astype(jnp.int32)].add(route_part.astype(jnp.float32), mode='drop')
        return ((token_acc, route_acc), jnp.stack([grad_gate, grad_up, grad_down], 0))
    start = (jnp.zeros((TOKENS, D), jnp.float32), jnp.zeros((sentinel,), jnp.float32))
    (token_acc, route_acc), grads = lax.scan(per_expert, start, (weights, table))
    param_count = 3.0 * EXPERTS * D * HID
    root_mean = jnp.sqrt(jnp.sum(grads * grads) / param_count + 1e-06)
    clip_factor = jnp.minimum(1.0, 0.5 / root_mean)
    clipped = clip_factor * grads
    first_next = 0.9 * first_moment.astype(jnp.float32) + 0.1 * clipped
    second_next = 0.95 * second_moment.astype(jnp.float32) + 0.05 * clipped * clipped
    update = first_next / (1.0 - 0.9 ** ADAM_STEP) / (jnp.sqrt(second_next / (1.0 - 0.95 ** ADAM_STEP)) + 1e-08)
    token_grad = token_acc.astype(jnp.bfloat16)
    routing_grad = route_acc.reshape(TOKENS, TOPK).astype(jnp.bfloat16)
    return (token_grad, routing_grad, first_next.astype(jnp.bfloat16), second_next.astype(jnp.bfloat16), update.astype(jnp.bfloat16))
```

```python
import jax
import jax.numpy as jnp
from jax import lax
from jax.experimental.layout import Layout, with_layout_constraint
from jax.sharding import Mesh, PartitionSpec as P

ADAM_STEP = 10
CORES = 2
BF16 = jnp.bfloat16
F32 = jnp.float32
INFO = 128


def plane(mesh):
    dp, ep = mesh.devices.shape
    y = 4
    z = ep // (y * CORES)
    return Mesh(mesh.devices.reshape(dp, y, z, CORES), ("x", "y", "z", "c"))


def on_device(tokens, cotangent, expert_ids, route_weights, weights, first_moment, second_moment):
    tok_count, model_width = tokens.shape
    topk_count = expert_ids.shape[1]
    hidden_units = weights.shape[3]
    ny, nz, nc = lax.axis_size("y"), lax.axis_size("z"), lax.axis_size("c")
    experts = ny * nz * nc
    capacity = (tok_count * topk_count * 9 + 8 * experts - 1) // (8 * experts)
    dests = ny * nc
    slots = nz * capacity
    yi, zi, ci = lax.axis_index("y"), lax.axis_index("z"), lax.axis_index("c")
    me = ((yi * nz + zi) * nc + ci).astype(F32)

    info = jnp.concatenate([expert_ids.astype(BF16), route_weights], 1)
    info = jnp.pad(info, ((0, 0), (0, INFO - 2 * topk_count)))
    info = with_layout_constraint(info, Layout((0, 1)))
    rows = with_layout_constraint(jnp.concatenate([tokens, info], 1), Layout((0, 1)))
    all_x = lax.all_gather(rows, "z", axis=0, tiled=True)
    all_cot = lax.all_gather(cotangent, "z", axis=0, tiled=True)

    ids = all_x[:, model_width : model_width + topk_count].astype(F32)
    dest = jnp.arange(dests, dtype=jnp.int32)
    dest_expert = (((dest // nc) * nz + zi) * nc + dest % nc).astype(F32)
    match = jnp.any(ids[:, :, None] == dest_expert[None, None, :], 1)
    tri = jnp.tril(jnp.ones((tok_count, tok_count), BF16))
    count = jnp.einsum(
        "ab,sbd->sad", tri, match.astype(BF16).reshape(nz, tok_count, dests), preferred_element_type=F32
    )
    base = (jnp.arange(nz, dtype=jnp.int32) * capacity - 1).astype(F32)[:, None, None]
    slot = jnp.where(match, (count + base).reshape(nz * tok_count, dests), -1.0)
    slot = lax.optimization_barrier(slot.T)
    picks = (slot[:, None, :] == jnp.arange(slots, dtype=jnp.int32).astype(F32)[None, :, None]).astype(BF16)
    picks = lax.optimization_barrier(picks.reshape(dests * slots, nz * tok_count))

    def exchange(rows):
        width = rows.shape[1]
        out = lax.all_to_all(rows.reshape(dests, slots, width), ("y", "c"), split_axis=0, concat_axis=0, tiled=True)
        return out.reshape(dests * slots, width)

    recv = exchange(jnp.dot(picks, all_x, preferred_element_type=F32).astype(BF16))
    recv_cot = exchange(jnp.dot(picks, all_cot, preferred_element_type=F32).astype(BF16))
    recv_x = recv[:, :model_width]
    recv_ids = recv[:, model_width : model_width + topk_count].astype(F32)
    recv_rw = recv[:, model_width + topk_count : model_width + 2 * topk_count].astype(F32)
    mine = recv_ids == me
    row_weight = jnp.sum(jnp.where(mine, recv_rw, 0.0), 1, keepdims=True)

    w_gate, w_up, w_down = weights[0, 0], weights[0, 1], weights[0, 2]
    gate_val = jnp.dot(recv_x, w_gate, preferred_element_type=F32)
    up_val = jnp.dot(recv_x, w_up, preferred_element_type=F32)
    sigmoid_gate = jax.nn.sigmoid(gate_val)
    activated = gate_val * sigmoid_gate
    hidden = lax.optimization_barrier((activated * up_val).astype(BF16))
    back_val = jnp.dot(recv_cot, w_down, preferred_element_type=F32)
    route_part = jnp.sum(hidden.astype(F32) * back_val, 1, keepdims=True).astype(BF16)
    scaled = row_weight * back_val
    dgate = (scaled * up_val * sigmoid_gate * (1.0 + gate_val * (1.0 - sigmoid_gate))).astype(BF16)
    dup = (scaled * activated).astype(BF16)
    down_cot = (row_weight * recv_cot.astype(F32)).astype(BF16)
    slot_back = jnp.einsum("rh,dh->rd", dgate, w_gate, preferred_element_type=F32)
    slot_back = slot_back + jnp.einsum("rh,dh->rd", dup, w_up, preferred_element_type=F32)
    route_rows = jnp.where(mine, route_part, jnp.zeros((), BF16))
    route_rows = jnp.pad(route_rows, ((0, 0), (0, INFO - topk_count)))
    send_back = jnp.concatenate([slot_back.astype(BF16), route_rows], 1)
    send_back, grad_x, grad_cot = lax.optimization_barrier((send_back, recv_x, down_cot))
    back_rows = exchange(send_back)
    partial = lax.dot_general(picks, back_rows, (((0,), (0,)), ((), ())), preferred_element_type=F32)
    total = lax.psum_scatter(partial.astype(BF16), "z", scatter_dimension=0, tiled=True)
    token_grad = total[:, :model_width]
    routing_grad = total[:, model_width : model_width + topk_count]

    grad_local = jnp.stack(
        [
            jnp.einsum("rd,rh->dh", grad_x, dgate, preferred_element_type=F32).astype(BF16),
            jnp.einsum("rd,rh->dh", grad_x, dup, preferred_element_type=F32).astype(BF16),
            jnp.einsum("rd,rh->dh", grad_cot, hidden, preferred_element_type=F32).astype(BF16),
        ],
        0,
    )
    grad_share = lax.psum_scatter(grad_local, "x", scatter_dimension=1, tiled=True).astype(F32)[None]
    square = jnp.sum(grad_share * grad_share)
    square = jnp.broadcast_to(square, (experts, 1, 128))
    square = lax.all_to_all(square, ("y", "z", "c"), split_axis=0, concat_axis=0, tiled=True)
    square_sum = lax.psum(jnp.sum(square[:, 0, 0]), "x")
    param_count = 3.0 * experts * model_width * hidden_units
    root_mean = jnp.sqrt(square_sum / param_count + 1e-06)
    clip_factor = jnp.minimum(1.0, 0.5 / root_mean)
    clipped = clip_factor * grad_share
    first_next = 0.9 * first_moment.astype(F32) + 0.1 * clipped
    second_next = 0.95 * second_moment.astype(F32) + 0.05 * clipped * clipped
    update = (
        first_next
        / (1.0 - 0.9**ADAM_STEP)
        / (jnp.sqrt(second_next / (1.0 - 0.95**ADAM_STEP)) + 1e-08)
    )
    return (
        token_grad,
        routing_grad,
        first_next.astype(BF16),
        second_next.astype(BF16),
        update.astype(BF16),
    )


def solution(mesh):
    tok = P(("x", "y", "z", "c"), None)
    ep = ("y", "z", "c")
    state = P(ep, None, "x", None)
    return jax.shard_map(
        on_device,
        mesh=plane(mesh),
        in_specs=(tok, tok, tok, tok, P(ep, None, None, None), state, state),
        out_specs=(tok, tok, state, state, state),
        check_vma=False,
    )
```

```python
import jax
import jax.numpy as jnp
from jax import lax
from jax.experimental.layout import Layout, with_layout_constraint
from jax.sharding import Mesh, PartitionSpec as P

ADAM_STEP = 10
CORES = 2
BF16 = jnp.bfloat16
F32 = jnp.float32
INFO = 128


def plane(mesh):
    dp, ep = mesh.devices.shape
    y = 4
    z = ep // (y * CORES)
    return Mesh(mesh.devices.reshape(dp, y, z, CORES), ("x", "y", "z", "c"))


def on_device(tokens, cotangent, expert_ids, route_weights, weights, first_moment, second_moment):
    tok_count, model_width = tokens.shape
    topk_count = expert_ids.shape[1]
    hidden_units = weights.shape[3]
    ny, nz, nc = lax.axis_size("y"), lax.axis_size("z"), lax.axis_size("c")
    experts = ny * nz * nc
    capacity = (tok_count * topk_count * 9 + 8 * experts - 1) // (8 * experts)
    dests = ny * nc
    yi, zi, ci = lax.axis_index("y"), lax.axis_index("z"), lax.axis_index("c")
    me = ((yi * nz + zi) * nc + ci).astype(F32)

    info = jnp.concatenate([expert_ids.astype(BF16), route_weights], 1)
    info = jnp.pad(info, ((0, 0), (0, INFO - 2 * topk_count)))
    info = with_layout_constraint(info, Layout((0, 1)))
    rows = with_layout_constraint(jnp.concatenate([tokens, info], 1), Layout((0, 1)))

    def shift(block, step):
        return lax.ppermute(block, "z", [(i, (i + step) % nz) for i in range(nz)])

    half = tok_count // 2
    far = nz // 2

    def ring(block):
        ups, downs = [block], [block]
        for _ in range(1, far):
            up = shift(ups[-1], 1)
            down = shift(downs[-1], -1)
            ups.append(up)
            downs.append(down)
        up = shift(ups[-1][:half], 1)
        down = shift(downs[-1][half:], -1)
        ups.append(jnp.concatenate([up, down], 0))
        near = [ups[0], ups[1], downs[1], ups[2]]
        away = [downs[2], ups[3], downs[3], ups[4]]
        return near, away

    x_groups = ring(rows)
    cot_groups = ring(cotangent)
    group = len(x_groups[0])
    slots = group * capacity
    dest = jnp.arange(dests, dtype=jnp.int32)
    dest_expert = (((dest // nc) * nz + zi) * nc + dest % nc).astype(F32)
    tri = jnp.tril(jnp.ones((tok_count, tok_count), BF16))
    base = (jnp.arange(group, dtype=jnp.int32) * capacity - 1).astype(F32)[:, None, None]

    def pick_matrix(blocks):
        ids = jnp.concatenate([b[:, model_width : model_width + topk_count] for b in blocks], 0).astype(F32)
        match = jnp.any(ids[:, :, None] == dest_expert[None, None, :], 1)
        count = jnp.einsum(
            "ab,sbd->sad", tri, match.astype(BF16).reshape(group, tok_count, dests), preferred_element_type=F32
        )
        slot = jnp.where(match, (count + base).reshape(group * tok_count, dests), -1.0)
        slot = lax.optimization_barrier(slot.T)
        place = jnp.arange(slots, dtype=jnp.int32).astype(F32)[None, :, None]
        picks = (slot[:, None, :] == place).astype(BF16)
        return lax.optimization_barrier(picks.reshape(dests * slots, group * tok_count))

    def exchange(rows):
        width = rows.shape[1]
        out = lax.all_to_all(rows.reshape(dests, slots, width), ("y", "c"), split_axis=0, concat_axis=0, tiled=True)
        return out.reshape(dests * slots, width)

    def select(picks, blocks):
        return jnp.dot(picks, jnp.concatenate(blocks, 0), preferred_element_type=F32).astype(BF16)

    near_picks = pick_matrix(x_groups[0])
    near_rows = select(near_picks, x_groups[0])
    near_recv = exchange(near_rows)
    *away_blocks, _ = lax.optimization_barrier((*x_groups[1], near_rows))
    away_picks = pick_matrix(away_blocks)
    away_rows = select(away_picks, away_blocks)
    away_recv = exchange(away_rows)
    away_cot = exchange(select(away_picks, cot_groups[1]))
    near_cot = exchange(select(near_picks, cot_groups[0]))
    picks = [near_picks, away_picks]

    w_gate, w_up, w_down = weights[0, 0], weights[0, 1], weights[0, 2]

    def expert(recv, recv_cot):
        recv_x = recv[:, :model_width]
        recv_ids = recv[:, model_width : model_width + topk_count].astype(F32)
        recv_rw = recv[:, model_width + topk_count : model_width + 2 * topk_count].astype(F32)
        mine = recv_ids == me
        row_weight = jnp.sum(jnp.where(mine, recv_rw, 0.0), 1, keepdims=True)
        gate_val = jnp.dot(recv_x, w_gate, preferred_element_type=F32)
        up_val = jnp.dot(recv_x, w_up, preferred_element_type=F32)
        sigmoid_gate = jax.nn.sigmoid(gate_val)
        activated = gate_val * sigmoid_gate
        hidden = lax.optimization_barrier((activated * up_val).astype(BF16))
        back_val = jnp.dot(recv_cot, w_down, preferred_element_type=F32)
        route_part = jnp.sum(hidden.astype(F32) * back_val, 1, keepdims=True).astype(BF16)
        scaled = row_weight * back_val
        dgate = (scaled * up_val * sigmoid_gate * (1.0 + gate_val * (1.0 - sigmoid_gate))).astype(BF16)
        dup = (scaled * activated).astype(BF16)
        down_cot = (row_weight * recv_cot.astype(F32)).astype(BF16)
        slot_back = jnp.einsum("rh,dh->rd", dgate, w_gate, preferred_element_type=F32)
        slot_back = slot_back + jnp.einsum("rh,dh->rd", dup, w_up, preferred_element_type=F32)
        route_rows = jnp.where(mine, route_part, jnp.zeros((), BF16))
        route_rows = jnp.pad(route_rows, ((0, 0), (0, INFO - topk_count)))
        send_back = jnp.concatenate([slot_back.astype(BF16), route_rows], 1)
        return send_back, recv_x, down_cot, dgate, dup, hidden

    def weight_grads(recv_x, down_cot, dgate, dup, hidden):
        return [
            jnp.einsum("rd,rh->dh", a, b, preferred_element_type=F32)
            for a, b in ((recv_x, dgate), (recv_x, dup), (down_cot, hidden))
        ]

    away_back, *away_work = expert(away_recv, away_cot)
    away_grads = weight_grads(*away_work)
    near_back, *near_work = expert(near_recv, near_cot)
    near_back, *near_work = lax.optimization_barrier((near_back, *near_work))
    near_grads = weight_grads(*near_work)

    def combine(picks, rows):
        out = lax.dot_general(picks, rows, (((0,), (0,)), ((), ())), preferred_element_type=F32).astype(BF16)
        return [out[i * tok_count : (i + 1) * tok_count] for i in range(group)]

    def add(a, b):
        return (a.astype(F32) + b.astype(F32)).astype(BF16)

    away_ret = exchange(away_back)
    near_ret = exchange(near_back)
    part = {}
    part[2], part[-3], part[3], part[4] = combine(picks[1], away_ret)
    part[0], part[-1], part[1], part[-2] = combine(picks[0], near_ret)
    up = shift(part[4][:half], 1)
    down = shift(part[4][half:], -1)
    up = shift(jnp.concatenate([add(part[3][:half], up), part[3][half:]], 0), 1)
    down = shift(jnp.concatenate([part[-3][:half], add(part[-3][half:], down)], 0), -1)
    for k in range(far - 2, 0, -1):
        up = shift(add(part[k], up), 1)
        down = shift(add(part[-k], down), -1)
    total = part[0].astype(F32) + up.astype(F32) + down.astype(F32)
    token_grad = total[:, :model_width].astype(BF16)
    routing_grad = total[:, model_width : model_width + topk_count].astype(BF16)

    grad_local = jnp.stack([(a + b).astype(BF16) for a, b in zip(near_grads, away_grads)], 0)
    grad_share = lax.psum_scatter(grad_local, "x", scatter_dimension=1, tiled=True).astype(F32)[None]
    square = jnp.sum(grad_share * grad_share)
    square = jnp.broadcast_to(square, (lax.axis_size("x") * experts, 1, 128))
    square = lax.all_to_all(square, ("x", "y", "z", "c"), split_axis=0, concat_axis=0, tiled=True)
    square_sum = jnp.sum(square[:, 0, 0])
    param_count = 3.0 * experts * model_width * hidden_units
    root_mean = jnp.sqrt(square_sum / param_count + 1e-06)
    clip_factor = jnp.minimum(1.0, 0.5 / root_mean)
    clipped = clip_factor * grad_share
    first_next = 0.9 * first_moment.astype(F32) + 0.1 * clipped
    second_next = 0.95 * second_moment.astype(F32) + 0.05 * clipped * clipped
    update = (
        first_next
        / (1.0 - 0.9**ADAM_STEP)
        / (jnp.sqrt(second_next / (1.0 - 0.95**ADAM_STEP)) + 1e-08)
    )
    return (
        token_grad,
        routing_grad,
        first_next.astype(BF16),
        second_next.astype(BF16),
        update.astype(BF16),
    )


def solution(mesh):
    tok = P(("x", "y", "z", "c"), None)
    ep = ("y", "z", "c")
    state = P(ep, None, "x", None)

    return jax.shard_map(
        on_device,
        mesh=plane(mesh),
        in_specs=(tok, tok, tok, tok, P(ep, None, None, None), state, state),
        out_specs=(tok, tok, state, state, state),
        check_vma=False,
    )
```

```python
import jax
import jax.numpy as jnp
from jax import lax
from jax.experimental.layout import Layout, with_layout_constraint
from jax.sharding import Mesh, PartitionSpec as P

ADAM_STEP = 10
CORES = 2
BF16 = jnp.bfloat16
F32 = jnp.float32
INFO = 128


def plane(mesh):
    dp, ep = mesh.devices.shape
    y = 4
    z = ep // (y * CORES)
    return Mesh(mesh.devices.reshape(dp, y, z, CORES), ("x", "y", "z", "c"))


def on_device(tokens, cotangent, expert_ids, route_weights, weights, first_moment, second_moment):
    tok_count, model_width = tokens.shape
    topk_count = expert_ids.shape[1]
    hidden_units = weights.shape[3]
    ny, nz, nc = lax.axis_size("y"), lax.axis_size("z"), lax.axis_size("c")
    experts = ny * nz * nc
    capacity = (tok_count * topk_count * 9 + 8 * experts - 1) // (8 * experts)
    dests = ny * nc
    yi, zi, ci = lax.axis_index("y"), lax.axis_index("z"), lax.axis_index("c")
    me = ((yi * nz + zi) * nc + ci).astype(F32)

    info = jnp.concatenate([expert_ids.astype(BF16), route_weights], 1)
    info = jnp.pad(info, ((0, 0), (0, INFO - 2 * topk_count)))
    info = with_layout_constraint(info, Layout((0, 1)))
    rows = with_layout_constraint(jnp.concatenate([tokens, info], 1), Layout((0, 1)))

    def shift(block, step):
        return lax.ppermute(block, "z", [(i, (i + step) % nz) for i in range(nz)])

    half = tok_count // 2
    far = nz // 2

    def ring(block):
        ups, downs = [block], [block]
        for _ in range(1, far):
            up = shift(ups[-1], 1)
            down = shift(downs[-1], -1)
            ups.append(up)
            downs.append(down)
        up = shift(ups[-1][:half], 1)
        down = shift(downs[-1][half:], -1)
        ups.append(jnp.concatenate([up, down], 0))
        near = [ups[0], ups[1], downs[1], ups[2]]
        away = [downs[2], ups[3], downs[3], ups[4]]
        return near, away

    x_groups = ring(rows)
    cot_groups = ring(cotangent)
    group = len(x_groups[0])
    slots = group * capacity
    dest = jnp.arange(dests, dtype=jnp.int32)
    dest_expert = (((dest // nc) * nz + zi) * nc + dest % nc).astype(F32)
    tri = jnp.tril(jnp.ones((tok_count, tok_count), BF16))
    base = (jnp.arange(group, dtype=jnp.int32) * capacity - 1).astype(F32)[:, None, None]

    def pick_matrix(blocks):
        ids = jnp.concatenate([b[:, model_width : model_width + topk_count] for b in blocks], 0).astype(F32)
        match = jnp.any(ids[:, :, None] == dest_expert[None, None, :], 1)
        count = jnp.einsum(
            "ab,sbd->sad", tri, match.astype(BF16).reshape(group, tok_count, dests), preferred_element_type=F32
        )
        slot = jnp.where(match, (count + base).reshape(group * tok_count, dests), -1.0)
        slot = lax.optimization_barrier(slot.T)
        place = jnp.arange(slots, dtype=jnp.int32).astype(F32)[None, :, None]
        picks = (slot[:, None, :] == place).astype(BF16)
        return lax.optimization_barrier(picks.reshape(dests * slots, group * tok_count))

    def exchange(rows):
        width = rows.shape[1]
        out = lax.all_to_all(rows.reshape(dests, slots, width), ("y", "c"), split_axis=0, concat_axis=0, tiled=True)
        return out.reshape(dests * slots, width)

    def select(picks, blocks):
        return jnp.dot(picks, jnp.concatenate(blocks, 0), preferred_element_type=F32).astype(BF16)

    near_picks = pick_matrix(x_groups[0])
    near_rows = select(near_picks, x_groups[0])
    near_recv = exchange(near_rows)
    *away_blocks, _ = lax.optimization_barrier((*x_groups[1], near_rows))
    away_picks = pick_matrix(away_blocks)
    away_rows = select(away_picks, away_blocks)
    away_recv = exchange(away_rows)
    away_cot = exchange(select(away_picks, cot_groups[1]))
    near_cot = exchange(select(near_picks, cot_groups[0]))
    picks = [near_picks, away_picks]

    w_gate, w_up, w_down = weights[0, 0], weights[0, 1], weights[0, 2]

    def expert(recv, recv_cot):
        recv_x = recv[:, :model_width]
        recv_ids = recv[:, model_width : model_width + topk_count].astype(F32)
        recv_rw = recv[:, model_width + topk_count : model_width + 2 * topk_count].astype(F32)
        mine = recv_ids == me
        row_weight = jnp.sum(jnp.where(mine, recv_rw, 0.0), 1, keepdims=True)
        gate_val = jnp.dot(recv_x, w_gate, preferred_element_type=F32)
        up_val = jnp.dot(recv_x, w_up, preferred_element_type=F32)
        sigmoid_gate = jax.nn.sigmoid(gate_val)
        activated = gate_val * sigmoid_gate
        hidden = lax.optimization_barrier((activated * up_val).astype(BF16))
        back_val = jnp.dot(recv_cot, w_down, preferred_element_type=F32)
        route_part = jnp.sum(hidden.astype(F32) * back_val, 1, keepdims=True).astype(BF16)
        scaled = row_weight * back_val
        dgate = (scaled * up_val * sigmoid_gate * (1.0 + gate_val * (1.0 - sigmoid_gate))).astype(BF16)
        dup = (scaled * activated).astype(BF16)
        down_cot = (row_weight * recv_cot.astype(F32)).astype(BF16)
        slot_back = jnp.einsum("rh,dh->rd", dgate, w_gate, preferred_element_type=F32)
        slot_back = slot_back + jnp.einsum("rh,dh->rd", dup, w_up, preferred_element_type=F32)
        route_rows = jnp.where(mine, route_part, jnp.zeros((), BF16))
        route_rows = jnp.pad(route_rows, ((0, 0), (0, INFO - topk_count)))
        send_back = jnp.concatenate([slot_back.astype(BF16), route_rows], 1)
        return send_back, recv_x, down_cot, dgate, dup, hidden

    def weight_grads(recv_x, down_cot, dgate, dup, hidden):
        return [
            jnp.einsum("rd,rh->dh", a, b, preferred_element_type=F32)
            for a, b in ((recv_x, dgate), (recv_x, dup), (down_cot, hidden))
        ]

    away_back, *away_work = expert(away_recv, away_cot)
    away_grads = lax.optimization_barrier(weight_grads(*away_work))
    near_cot, away_back = lax.optimization_barrier((near_cot, away_back))
    near_back, *near_work = expert(near_recv, near_cot)
    near_back, *near_work = lax.optimization_barrier((near_back, *near_work))
    near_grads = weight_grads(*near_work)

    def combine(picks, rows):
        out = lax.dot_general(picks, rows, (((0,), (0,)), ((), ())), preferred_element_type=F32).astype(BF16)
        return [out[i * tok_count : (i + 1) * tok_count] for i in range(group)]

    def add(a, b):
        return (a.astype(F32) + b.astype(F32)).astype(BF16)

    away_ret = exchange(away_back)
    near_ret = exchange(near_back)
    part = {}
    part[2], part[-3], part[3], part[4] = combine(picks[1], away_ret)
    part[0], part[-1], part[1], part[-2] = combine(picks[0], near_ret)
    up = shift(part[4][:half], 1)
    down = shift(part[4][half:], -1)
    up = shift(jnp.concatenate([add(part[3][:half], up), part[3][half:]], 0), 1)
    down = shift(jnp.concatenate([part[-3][:half], add(part[-3][half:], down)], 0), -1)
    for k in range(far - 2, 0, -1):
        up = shift(add(part[k], up), 1)
        down = shift(add(part[-k], down), -1)
    total = part[0].astype(F32) + up.astype(F32) + down.astype(F32)
    token_grad = total[:, :model_width].astype(BF16)
    routing_grad = total[:, model_width : model_width + topk_count].astype(BF16)

    grad_local = jnp.stack([(a + b).astype(BF16) for a, b in zip(near_grads, away_grads)], 0)
    nx = lax.axis_size("x")
    xi = lax.axis_index("x")
    width = model_width // nx
    owners = [jnp.where(xi + k >= nx, xi + k - nx, xi + k) for k in range(nx)]
    shares = [lax.dynamic_slice_in_dim(grad_local, owner * width, width, 1) for owner in owners]
    for k in range(1, nx):
        shares[k] = lax.ppermute(shares[k], "x", [(i, (i + k) % nx) for i in range(nx)])
    grad_share = sum(g.astype(F32) for g in shares)[None]
    square = jnp.sum(grad_share * grad_share)
    square = jnp.broadcast_to(square, (lax.axis_size("x") * experts, 1, 128))
    square = lax.all_to_all(square, ("x", "y", "z", "c"), split_axis=0, concat_axis=0, tiled=True)
    square_sum = jnp.sum(square[:, 0, 0])
    param_count = 3.0 * experts * model_width * hidden_units
    root_mean = jnp.sqrt(square_sum / param_count + 1e-06)
    clip_factor = jnp.minimum(1.0, 0.5 / root_mean)
    clipped = clip_factor * grad_share
    first_next = 0.9 * first_moment.astype(F32) + 0.1 * clipped
    second_next = 0.95 * second_moment.astype(F32) + 0.05 * clipped * clipped
    update = (
        first_next
        / (1.0 - 0.9**ADAM_STEP)
        / (jnp.sqrt(second_next / (1.0 - 0.95**ADAM_STEP)) + 1e-08)
    )
    return (
        token_grad,
        routing_grad,
        first_next.astype(BF16),
        second_next.astype(BF16),
        update.astype(BF16),
    )


def solution(mesh):
    tok = P(("x", "y", "z", "c"), None)
    ep = ("y", "z", "c")
    state = P(ep, None, "x", None)

    return jax.shard_map(
        on_device,
        mesh=plane(mesh),
        in_specs=(tok, tok, tok, tok, P(ep, None, None, None), state, state),
        out_specs=(tok, tok, state, state, state),
        check_vma=False,
    )
```

```python
import jax
import jax.numpy as jnp
from jax import lax
from jax.experimental import pallas as pl
from jax.experimental.pallas import tpu as pltpu
from jax.experimental.layout import Layout, with_layout_constraint
from jax.sharding import Mesh, PartitionSpec as P

ADAM_STEP = 10
CORES = 2
BF16 = jnp.bfloat16
F32 = jnp.float32
INFO = 128
LANES = 128


def plane(mesh):
    dp, ep = mesh.devices.shape
    y = 4
    z = ep // (y * CORES)
    return Mesh(mesh.devices.reshape(dp, y, z, CORES), ("x", "y", "z", "c"))


def on_device(tokens, cotangent, expert_ids, route_weights, weights, first_moment, second_moment):
    tok_count, model_width = tokens.shape
    topk_count = expert_ids.shape[1]
    hidden_units = weights.shape[3]
    ny, nz, nc = lax.axis_size("y"), lax.axis_size("z"), lax.axis_size("c")
    experts = ny * nz * nc
    capacity = (tok_count * topk_count * 9 + 8 * experts - 1) // (8 * experts)
    dests = ny * nc
    yi, zi, ci = lax.axis_index("y"), lax.axis_index("z"), lax.axis_index("c")
    me = ((yi * nz + zi) * nc + ci).astype(F32)

    info = jnp.concatenate([expert_ids.astype(BF16), route_weights], 1)
    info = jnp.pad(info, ((0, 0), (0, INFO - 2 * topk_count)))
    info = with_layout_constraint(info, Layout((0, 1)))
    rows = with_layout_constraint(jnp.concatenate([tokens, info], 1), Layout((0, 1)))

    def shift(block, step):
        return lax.ppermute(block, "z", [(i, (i + step) % nz) for i in range(nz)])

    half = tok_count // 2
    far = nz // 2

    def ring(block):
        ups, downs = [block], [block]
        for _ in range(1, far):
            up = shift(ups[-1], 1)
            down = shift(downs[-1], -1)
            ups.append(up)
            downs.append(down)
        up = shift(ups[-1][:half], 1)
        down = shift(downs[-1][half:], -1)
        ups.append(jnp.concatenate([up, down], 0))
        near = [ups[0], ups[1], downs[1], ups[2]]
        away = [downs[2], ups[3], downs[3], ups[4]]
        return near, away

    x_groups = ring(rows)
    cot_groups = ring(cotangent)
    group = len(x_groups[0])
    slots = group * capacity
    dest = jnp.arange(dests, dtype=jnp.int32)
    dest_expert = (((dest // nc) * nz + zi) * nc + dest % nc).astype(F32)
    tri = jnp.tril(jnp.ones((tok_count, tok_count), BF16))
    base = (jnp.arange(group, dtype=jnp.int32) * capacity - 1).astype(F32)[:, None, None]

    def pick_matrix(blocks):
        ids = jnp.concatenate([b[:, model_width : model_width + topk_count] for b in blocks], 0).astype(F32)
        match = jnp.any(ids[:, :, None] == dest_expert[None, None, :], 1)
        count = jnp.einsum(
            "ab,sbd->sad", tri, match.astype(BF16).reshape(group, tok_count, dests), preferred_element_type=F32
        )
        slot = jnp.where(match, (count + base).reshape(group * tok_count, dests), -1.0)
        slot = lax.optimization_barrier(slot.T)
        place = jnp.arange(slots, dtype=jnp.int32).astype(F32)[None, :, None]
        picks = (slot[:, None, :] == place).astype(BF16)
        return lax.optimization_barrier(picks.reshape(dests * slots, group * tok_count))

    def exchange(rows):
        width = rows.shape[1]
        out = lax.all_to_all(rows.reshape(dests, slots, width), ("y", "c"), split_axis=0, concat_axis=0, tiled=True)
        return out.reshape(dests * slots, width)

    def select(picks, blocks):
        return jnp.dot(picks, jnp.concatenate(blocks, 0), preferred_element_type=F32).astype(BF16)

    near_picks = pick_matrix(x_groups[0])
    near_rows = select(near_picks, x_groups[0])
    near_recv = exchange(near_rows)
    *away_blocks, _ = lax.optimization_barrier((*x_groups[1], near_rows))
    away_picks = pick_matrix(away_blocks)
    away_rows = select(away_picks, away_blocks)
    away_recv = exchange(away_rows)
    away_cot = exchange(select(away_picks, cot_groups[1]))
    near_cot = exchange(select(near_picks, cot_groups[0]))
    picks = [near_picks, away_picks]

    w_gate, w_up, w_down = weights[0, 0], weights[0, 1], weights[0, 2]

    def expert(recv, recv_cot):
        recv_x = recv[:, :model_width]
        recv_ids = recv[:, model_width : model_width + topk_count].astype(F32)
        recv_rw = recv[:, model_width + topk_count : model_width + 2 * topk_count].astype(F32)
        mine = recv_ids == me
        row_weight = jnp.sum(jnp.where(mine, recv_rw, 0.0), 1, keepdims=True)
        gate_val = jnp.dot(recv_x, w_gate, preferred_element_type=F32)
        up_val = jnp.dot(recv_x, w_up, preferred_element_type=F32)
        sigmoid_gate = jax.nn.sigmoid(gate_val)
        activated = gate_val * sigmoid_gate
        hidden = lax.optimization_barrier((activated * up_val).astype(BF16))
        back_val = jnp.dot(recv_cot, w_down, preferred_element_type=F32)
        route_part = jnp.sum(hidden.astype(F32) * back_val, 1, keepdims=True).astype(BF16)
        scaled = row_weight * back_val
        dgate = (scaled * up_val * sigmoid_gate * (1.0 + gate_val * (1.0 - sigmoid_gate))).astype(BF16)
        dup = (scaled * activated).astype(BF16)
        down_cot = (row_weight * recv_cot.astype(F32)).astype(BF16)
        return (dgate, dup, route_part, mine), (recv_x, down_cot, dgate, dup, hidden)

    def rows_back(dgate, dup, route_part, mine):
        slot_back = jnp.einsum("rh,dh->rd", dgate, w_gate, preferred_element_type=F32)
        slot_back = slot_back + jnp.einsum("rh,dh->rd", dup, w_up, preferred_element_type=F32)
        route_rows = jnp.where(mine, route_part, jnp.zeros((), BF16))
        route_rows = jnp.pad(route_rows, ((0, 0), (0, INFO - topk_count)))
        return jnp.concatenate([slot_back.astype(BF16), route_rows], 1)

    def weight_grads(recv_x, down_cot, dgate, dup, hidden):
        return [
            jnp.einsum("rd,rh->dh", a, b, preferred_element_type=F32)
            for a, b in ((recv_x, dgate), (recv_x, dup), (down_cot, hidden))
        ]

    away_slots, away_work = expert(away_recv, away_cot)
    away_back = rows_back(*away_slots)
    away_grads = lax.optimization_barrier(weight_grads(*away_work))
    near_cot, away_back = lax.optimization_barrier((near_cot, away_back))
    near_slots, near_work = expert(near_recv, near_cot)
    nx = lax.axis_size("x")
    xi = lax.axis_index("x")
    width = model_width // nx
    near_grads = weight_grads(*near_work)
    near_grads = [(a + b).astype(BF16) for a, b in zip(near_grads, away_grads)]
    owners = [jnp.where(xi + k >= nx, xi + k - nx, xi + k) for k in range(nx)]
    grad_local = jnp.stack(near_grads, 0)
    shares = [lax.dynamic_slice_in_dim(grad_local, owner * width, width, 1) for owner in owners]
    near_slots, shares = lax.optimization_barrier((near_slots, shares))
    near_back = rows_back(*near_slots)

    def combine(picks, rows):
        out = lax.dot_general(picks, rows, (((0,), (0,)), ((), ())), preferred_element_type=F32).astype(BF16)
        return [out[i * tok_count : (i + 1) * tok_count] for i in range(group)]

    def add(a, b):
        return (a.astype(F32) + b.astype(F32)).astype(BF16)

    away_ret = exchange(away_back)
    near_ret = exchange(near_back)
    part = {}
    part[2], part[-3], part[3], part[4] = combine(picks[1], away_ret)
    part[0], part[-1], part[1], part[-2] = combine(picks[0], near_ret)
    up = shift(part[4][:half], 1)
    down = shift(part[4][half:], -1)
    up = shift(jnp.concatenate([add(part[3][:half], up), part[3][half:]], 0), 1)
    down = shift(jnp.concatenate([part[-3][:half], add(part[-3][half:], down)], 0), -1)
    up_part, down_part = part[far - 2], part[2 - far]
    for k in range(far - 2, 0, -1):
        up_sum = add(up_part, up)
        up = shift(up_sum, 1)
        down_sum = add(down_part, down)
        down = shift(down_sum, -1)
        up_part, down_part, _, _ = lax.optimization_barrier((part[k - 1], part[1 - k], up_sum, down_sum))
    total = up_part.astype(F32) + up.astype(F32) + down.astype(F32)
    token_grad = total[:, :model_width].astype(BF16)
    routing_grad = total[:, model_width : model_width + topk_count].astype(BF16)

    for k in range(1, nx):
        shares[k] = lax.ppermute(shares[k], "x", [(i, (i + k) % nx) for i in range(nx)])
    state_shape = (3 * width, hidden_units)
    grad_sum, square = sum_shares([g.reshape(state_shape) for g in shares])
    square = lax.all_to_all(square, ("x", "y"), split_axis=0, concat_axis=0, tiled=True)
    square = jnp.broadcast_to(jnp.sum(square, 0, keepdims=True), (nz * nc, LANES))
    square = lax.all_to_all(square, ("z", "c"), split_axis=0, concat_axis=0, tiled=True)
    param_count = 3.0 * experts * model_width * hidden_units
    states = adam(param_count, square, grad_sum, first_moment.reshape(state_shape), second_moment.reshape(state_shape))
    return (token_grad, routing_grad, *(a.reshape(first_moment.shape) for a in states))


def sum_shares(shares):
    rows, hidden = shares[0].shape
    peers = lax.axis_size("x") * lax.axis_size("y")
    block = rows // 4

    def kernel(*refs):
        *parts, grad_ref, square_ref, acc = refs
        step = pl.program_id(0)
        grad = sum(part[...].astype(F32) for part in parts)
        grad_ref[...] = grad
        squares = jnp.sum((grad * grad).reshape(block // 8, 8, hidden), 0)

        @pl.when(step == 0)
        def _():
            acc[...] = squares

        @pl.when(step > 0)
        def _():
            acc[...] += squares

        @pl.when(step == pl.num_programs(0) - 1)
        def _():
            total = jnp.sum(jnp.sum(acc[...], 0, keepdims=True), 1, keepdims=True)
            square_ref[...] = jnp.broadcast_to(total, square_ref.shape)

    spec = pl.BlockSpec((block, hidden), lambda i: (i, 0))
    return pl.pallas_call(
        kernel,
        out_shape=(jax.ShapeDtypeStruct((rows, hidden), F32), jax.ShapeDtypeStruct((peers, LANES), F32)),
        grid=(rows // block,),
        in_specs=[spec] * len(shares),
        out_specs=(spec, pl.BlockSpec((peers, LANES), lambda i: (0, 0))),
        scratch_shapes=[pltpu.VMEM((8, hidden), F32)],
        cost_estimate=pl.CostEstimate(flops=7 * rows * hidden, bytes_accessed=12 * rows * hidden, transcendentals=0),
        name="sum_shares",
    )(*shares)


def adam(param_count, square, grads, first, second):
    rows, hidden = grads.shape
    block = rows // 6

    def kernel(square_ref, grad_ref, first_ref, second_ref, new_first_ref, new_second_ref, update_ref):
        square_sum = jnp.sum(square_ref[...], 0, keepdims=True)[:, :1]
        root_mean = jnp.sqrt(square_sum / param_count + 1e-06)
        clip_factor = jnp.minimum(1.0, 0.5 / root_mean)
        clipped = clip_factor * grad_ref[...]
        first_next = 0.9 * first_ref[...].astype(F32) + 0.1 * clipped
        second_next = 0.95 * second_ref[...].astype(F32) + 0.05 * clipped * clipped
        update = (
            first_next
            / (1.0 - 0.9**ADAM_STEP)
            / (jnp.sqrt(second_next / (1.0 - 0.95**ADAM_STEP)) + 1e-08)
        )
        new_first_ref[...] = first_next.astype(BF16)
        new_second_ref[...] = second_next.astype(BF16)
        update_ref[...] = update.astype(BF16)

    spec = pl.BlockSpec((block, hidden), lambda i: (i, 0))
    return pl.pallas_call(
        kernel,
        out_shape=[jax.ShapeDtypeStruct((rows, hidden), BF16)] * 3,
        grid=(rows // block,),
        in_specs=[pl.BlockSpec(square.shape, lambda i: (0, 0))] + [spec] * 3,
        out_specs=[spec] * 3,
        cost_estimate=pl.CostEstimate(
            flops=16 * rows * hidden, bytes_accessed=14 * rows * hidden, transcendentals=rows * hidden
        ),
        name="adam",
    )(square, grads, first, second)


def solution(mesh):
    tok = P(("x", "y", "z", "c"), None)
    ep = ("y", "z", "c")
    state = P(ep, None, "x", None)

    return jax.shard_map(
        on_device,
        mesh=plane(mesh),
        in_specs=(tok, tok, tok, tok, P(ep, None, None, None), state, state),
        out_specs=(tok, tok, state, state, state),
        check_vma=False,
    )
```

```python
import jax
import jax.numpy as jnp
from jax import lax
from jax.experimental.layout import Layout, with_layout_constraint
from jax.sharding import Mesh, PartitionSpec as P

ADAM_STEP = 10
CORES = 2
BF16 = jnp.bfloat16
F32 = jnp.float32
INFO = 128


def plane(mesh):
    dp, ep = mesh.devices.shape
    y = 4
    z = ep // (y * CORES)
    return Mesh(mesh.devices.reshape(dp, y, z, CORES), ("x", "y", "z", "c"))


def on_device(tokens, cotangent, expert_ids, route_weights, weights, first_moment, second_moment):
    tok_count, model_width = tokens.shape
    topk_count = expert_ids.shape[1]
    hidden_units = weights.shape[3]
    ny, nz, nc = lax.axis_size("y"), lax.axis_size("z"), lax.axis_size("c")
    experts = ny * nz * nc
    capacity = (tok_count * topk_count * 9 + 8 * experts - 1) // (8 * experts)
    dests = ny * nc
    yi, zi, ci = lax.axis_index("y"), lax.axis_index("z"), lax.axis_index("c")
    me = ((yi * nz + zi) * nc + ci).astype(F32)

    info = jnp.concatenate([expert_ids.astype(BF16), route_weights], 1)
    info = jnp.pad(info, ((0, 0), (0, INFO - 2 * topk_count)))
    info = with_layout_constraint(info, Layout((0, 1)))
    rows = with_layout_constraint(jnp.concatenate([tokens, info], 1), Layout((0, 1)))

    def shift(block, step):
        return lax.ppermute(block, "z", [(i, (i + step) % nz) for i in range(nz)])

    half = tok_count // 2
    far = nz // 2

    def ring(block):
        ups, downs = [block], [block]
        for _ in range(1, far):
            up = shift(ups[-1], 1)
            down = shift(downs[-1], -1)
            ups.append(up)
            downs.append(down)
        up = shift(ups[-1][:half], 1)
        down = shift(downs[-1][half:], -1)
        ups.append(jnp.concatenate([up, down], 0))
        near = [ups[0], ups[1], downs[1], ups[2]]
        away = [downs[2], ups[3], downs[3], ups[4]]
        return near, away

    x_groups = ring(rows)
    cot_groups = ring(cotangent)
    group = len(x_groups[0])
    slots = group * capacity
    dest = jnp.arange(dests, dtype=jnp.int32)
    dest_expert = (((dest // nc) * nz + zi) * nc + dest % nc).astype(F32)
    tri = jnp.tril(jnp.ones((tok_count, tok_count), BF16))
    base = (jnp.arange(group, dtype=jnp.int32) * capacity - 1).astype(F32)[:, None, None]

    def pick_matrix(blocks):
        ids = jnp.concatenate([b[:, model_width : model_width + topk_count] for b in blocks], 0).astype(F32)
        match = jnp.any(ids[:, :, None] == dest_expert[None, None, :], 1)
        count = jnp.einsum(
            "ab,sbd->sad", tri, match.astype(BF16).reshape(group, tok_count, dests), preferred_element_type=F32
        )
        slot = jnp.where(match, (count + base).reshape(group * tok_count, dests), -1.0)
        slot = lax.optimization_barrier(slot.T)
        place = jnp.arange(slots, dtype=jnp.int32).astype(F32)[None, :, None]
        picks = (slot[:, None, :] == place).astype(BF16)
        return lax.optimization_barrier(picks.reshape(dests * slots, group * tok_count))

    def exchange(rows):
        width = rows.shape[1]
        out = lax.all_to_all(rows.reshape(dests, slots, width), ("y", "c"), split_axis=0, concat_axis=0, tiled=True)
        return out.reshape(dests * slots, width)

    def select(picks, blocks):
        return jnp.dot(picks, jnp.concatenate(blocks, 0), preferred_element_type=F32).astype(BF16)

    near_picks = pick_matrix(x_groups[0])
    near_rows = select(near_picks, x_groups[0])
    near_recv = exchange(near_rows)
    *away_blocks, _ = lax.optimization_barrier((*x_groups[1], near_rows))
    away_picks = pick_matrix(away_blocks)
    away_rows = select(away_picks, away_blocks)
    away_recv = exchange(away_rows)
    away_cot = exchange(select(away_picks, cot_groups[1]))
    near_cot = exchange(select(near_picks, cot_groups[0]))
    picks = [near_picks, away_picks]

    w_gate, w_up, w_down = weights[0, 0], weights[0, 1], weights[0, 2]

    def expert(recv, recv_cot):
        recv_x = recv[:, :model_width]
        recv_ids = recv[:, model_width : model_width + topk_count].astype(F32)
        recv_rw = recv[:, model_width + topk_count : model_width + 2 * topk_count].astype(F32)
        mine = recv_ids == me
        row_weight = jnp.sum(jnp.where(mine, recv_rw, 0.0), 1, keepdims=True)
        gate_val = jnp.dot(recv_x, w_gate, preferred_element_type=F32)
        up_val = jnp.dot(recv_x, w_up, preferred_element_type=F32)
        sigmoid_gate = jax.nn.sigmoid(gate_val)
        activated = gate_val * sigmoid_gate
        hidden = lax.optimization_barrier((activated * up_val).astype(BF16))
        back_val = jnp.dot(recv_cot, w_down, preferred_element_type=F32)
        route_part = jnp.sum(hidden.astype(F32) * back_val, 1, keepdims=True).astype(BF16)
        scaled = row_weight * back_val
        dgate = (scaled * up_val * sigmoid_gate * (1.0 + gate_val * (1.0 - sigmoid_gate))).astype(BF16)
        dup = (scaled * activated).astype(BF16)
        down_cot = (row_weight * recv_cot.astype(F32)).astype(BF16)
        return (dgate, dup, route_part, mine), (recv_x, down_cot, dgate, dup, hidden)

    def rows_back(dgate, dup, route_part, mine):
        slot_back = jnp.einsum("rh,dh->rd", dgate, w_gate, preferred_element_type=F32)
        slot_back = slot_back + jnp.einsum("rh,dh->rd", dup, w_up, preferred_element_type=F32)
        route_rows = jnp.where(mine, route_part, jnp.zeros((), BF16))
        route_rows = jnp.pad(route_rows, ((0, 0), (0, INFO - topk_count)))
        return jnp.concatenate([slot_back.astype(BF16), route_rows], 1)

    def weight_grads(recv_x, down_cot, dgate, dup, hidden):
        return [
            jnp.einsum("rd,rh->dh", a, b, preferred_element_type=F32)
            for a, b in ((recv_x, dgate), (recv_x, dup), (down_cot, hidden))
        ]

    away_slots, away_work = expert(away_recv, away_cot)
    away_back = rows_back(*away_slots)
    away_grads = lax.optimization_barrier(weight_grads(*away_work))
    near_cot, away_back = lax.optimization_barrier((near_cot, away_back))
    near_slots, near_work = expert(near_recv, near_cot)
    nx = lax.axis_size("x")
    xi = lax.axis_index("x")
    width = model_width // nx
    near_grads = weight_grads(*near_work)
    near_grads = [(a + b).astype(BF16) for a, b in zip(near_grads, away_grads)]
    owners = [jnp.where(xi + k >= nx, xi + k - nx, xi + k) for k in range(nx)]
    grad_local = jnp.stack(near_grads, 0)
    shares = [lax.dynamic_slice_in_dim(grad_local, owner * width, width, 1) for owner in owners]
    near_slots, shares = lax.optimization_barrier((near_slots, shares))
    near_back = rows_back(*near_slots)

    def combine(picks, rows):
        out = lax.dot_general(picks, rows, (((0,), (0,)), ((), ())), preferred_element_type=F32).astype(BF16)
        return [out[i * tok_count : (i + 1) * tok_count] for i in range(group)]

    def add(a, b):
        return (a.astype(F32) + b.astype(F32)).astype(BF16)

    away_ret = exchange(away_back)
    near_ret = exchange(near_back)
    part = {}
    part[2], part[-3], part[3], part[4] = combine(picks[1], away_ret)
    part[0], part[-1], part[1], part[-2] = combine(picks[0], near_ret)
    up = shift(part[4][:half], 1)
    down = shift(part[4][half:], -1)
    up = shift(jnp.concatenate([add(part[3][:half], up), part[3][half:]], 0), 1)
    down = shift(jnp.concatenate([part[-3][:half], add(part[-3][half:], down)], 0), -1)
    up_part, down_part = part[far - 2], part[2 - far]
    for k in range(far - 2, 0, -1):
        up_sum = add(up_part, up)
        up = shift(up_sum, 1)
        down_sum = add(down_part, down)
        down = shift(down_sum, -1)
        up_part, down_part, _, _ = lax.optimization_barrier((part[k - 1], part[1 - k], up_sum, down_sum))
    total = up_part.astype(F32) + up.astype(F32) + down.astype(F32)
    token_grad = total[:, :model_width].astype(BF16)
    routing_grad = total[:, model_width : model_width + topk_count].astype(BF16)

    for k in range(1, nx):
        shares[k] = lax.ppermute(shares[k], "x", [(i, (i + k) % nx) for i in range(nx)])
    grad_share = sum(g.astype(F32) for g in shares)[None]
    square = jnp.sum(grad_share * grad_share)
    square = jnp.broadcast_to(square, (lax.axis_size("x") * experts, 1, 128))
    square = lax.all_to_all(square, ("x", "y", "z", "c"), split_axis=0, concat_axis=0, tiled=True)
    square_sum = jnp.sum(square[:, 0, 0])
    param_count = 3.0 * experts * model_width * hidden_units
    root_mean = jnp.sqrt(square_sum / param_count + 1e-06)
    clip_factor = jnp.minimum(1.0, 0.5 / root_mean)
    clipped = clip_factor * grad_share
    first_next = 0.9 * first_moment.astype(F32) + 0.1 * clipped
    second_next = 0.95 * second_moment.astype(F32) + 0.05 * clipped * clipped
    update = (
        first_next
        / (1.0 - 0.9**ADAM_STEP)
        / (jnp.sqrt(second_next / (1.0 - 0.95**ADAM_STEP)) + 1e-08)
    )
    return (
        token_grad,
        routing_grad,
        first_next.astype(BF16),
        second_next.astype(BF16),
        update.astype(BF16),
    )


def solution(mesh):
    tok = P(("x", "y", "z", "c"), None)
    ep = ("y", "z", "c")
    state = P(ep, None, "x", None)

    return jax.shard_map(
        on_device,
        mesh=plane(mesh),
        in_specs=(tok, tok, tok, tok, P(ep, None, None, None), state, state),
        out_specs=(tok, tok, state, state, state),
        check_vma=False,
    )
```

```python
import jax
import jax.numpy as jnp
from jax import lax
from jax.experimental.layout import Layout, with_layout_constraint
from jax.sharding import Mesh, PartitionSpec as P

ADAM_STEP = 10
CORES = 2
BF16 = jnp.bfloat16
F32 = jnp.float32
INFO = 128


def plane(mesh):
    dp, ep = mesh.devices.shape
    y = 4
    z = ep // (y * CORES)
    return Mesh(mesh.devices.reshape(dp, y, z, CORES), ("x", "y", "z", "c"))


def on_device(tokens, cotangent, expert_ids, route_weights, weights, first_moment, second_moment):
    tok_count, model_width = tokens.shape
    topk_count = expert_ids.shape[1]
    hidden_units = weights.shape[3]
    ny, nz, nc = lax.axis_size("y"), lax.axis_size("z"), lax.axis_size("c")
    experts = ny * nz * nc
    capacity = (tok_count * topk_count * 9 + 8 * experts - 1) // (8 * experts)
    dests = ny * nc
    yi, zi, ci = lax.axis_index("y"), lax.axis_index("z"), lax.axis_index("c")
    me = ((yi * nz + zi) * nc + ci).astype(F32)

    info = jnp.concatenate([expert_ids.astype(BF16), route_weights], 1)
    info = jnp.pad(info, ((0, 0), (0, INFO - 2 * topk_count)))
    info = with_layout_constraint(info, Layout((0, 1)))
    rows = with_layout_constraint(jnp.concatenate([tokens, info], 1), Layout((0, 1)))

    def shift(block, step):
        return lax.ppermute(block, "z", [(i, (i + step) % nz) for i in range(nz)])

    half = tok_count // 2
    far = nz // 2

    def ring(block):
        ups, downs = [block], [block]
        for _ in range(1, far):
            up = shift(ups[-1], 1)
            down = shift(downs[-1], -1)
            ups.append(up)
            downs.append(down)
        up = shift(ups[-1][:half], 1)
        down = shift(downs[-1][half:], -1)
        ups.append(jnp.concatenate([up, down], 0))
        near = [ups[0], ups[1], downs[1], ups[2]]
        away = [downs[2], ups[3], downs[3], ups[4]]
        return near, away

    x_groups = ring(rows)
    cot_groups = ring(cotangent)
    group = len(x_groups[0])
    slots = group * capacity
    dest = jnp.arange(dests, dtype=jnp.int32)
    dest_expert = (((dest // nc) * nz + zi) * nc + dest % nc).astype(F32)
    tri = jnp.tril(jnp.ones((tok_count, tok_count), BF16))
    base = (jnp.arange(group, dtype=jnp.int32) * capacity - 1).astype(F32)[:, None, None]

    def pick_matrix(blocks):
        ids = jnp.concatenate([b[:, model_width : model_width + topk_count] for b in blocks], 0).astype(F32)
        match = jnp.any(ids[:, :, None] == dest_expert[None, None, :], 1)
        count = jnp.einsum(
            "ab,sbd->sad", tri, match.astype(BF16).reshape(group, tok_count, dests), preferred_element_type=F32
        )
        slot = jnp.where(match, (count + base).reshape(group * tok_count, dests), -1.0)
        slot = lax.optimization_barrier(slot.T)
        place = jnp.arange(slots, dtype=jnp.int32).astype(F32)[None, :, None]
        picks = (slot[:, None, :] == place).astype(BF16)
        return lax.optimization_barrier(picks.reshape(dests * slots, group * tok_count))

    def exchange(rows):
        width = rows.shape[1]
        out = lax.all_to_all(rows.reshape(dests, slots, width), ("y", "c"), split_axis=0, concat_axis=0, tiled=True)
        return out.reshape(dests * slots, width)

    def select(picks, blocks):
        return jnp.dot(picks, jnp.concatenate(blocks, 0), preferred_element_type=F32).astype(BF16)

    near_picks = pick_matrix(x_groups[0])
    near_rows = select(near_picks, x_groups[0])
    near_recv = exchange(near_rows)
    *away_blocks, _ = lax.optimization_barrier((*x_groups[1], near_rows))
    away_picks = pick_matrix(away_blocks)
    away_rows = select(away_picks, away_blocks)
    away_recv = exchange(away_rows)
    away_cot = exchange(select(away_picks, cot_groups[1]))
    near_cot = exchange(select(near_picks, cot_groups[0]))
    picks = [near_picks, away_picks]

    w_gate, w_up, w_down = weights[0, 0], weights[0, 1], weights[0, 2]

    def expert(recv, recv_cot):
        recv_x = recv[:, :model_width]
        recv_ids = recv[:, model_width : model_width + topk_count].astype(F32)
        recv_rw = recv[:, model_width + topk_count : model_width + 2 * topk_count].astype(F32)
        mine = recv_ids == me
        row_weight = jnp.sum(jnp.where(mine, recv_rw, 0.0), 1, keepdims=True)
        gate_val = jnp.dot(recv_x, w_gate, preferred_element_type=F32)
        up_val = jnp.dot(recv_x, w_up, preferred_element_type=F32)
        sigmoid_gate = jax.nn.sigmoid(gate_val)
        activated = gate_val * sigmoid_gate
        hidden = lax.optimization_barrier((activated * up_val).astype(BF16))
        back_val = jnp.dot(recv_cot, w_down, preferred_element_type=F32)
        route_part = jnp.sum(hidden.astype(F32) * back_val, 1, keepdims=True).astype(BF16)
        scaled = row_weight * back_val
        dgate = (scaled * up_val * sigmoid_gate * (1.0 + gate_val * (1.0 - sigmoid_gate))).astype(BF16)
        dup = (scaled * activated).astype(BF16)
        down_cot = (row_weight * recv_cot.astype(F32)).astype(BF16)
        return (dgate, dup, route_part, mine), (recv_x, down_cot, dgate, dup, hidden)

    def rows_back(dgate, dup, route_part, mine):
        slot_back = jnp.einsum("rh,dh->rd", dgate, w_gate, preferred_element_type=F32)
        slot_back = slot_back + jnp.einsum("rh,dh->rd", dup, w_up, preferred_element_type=F32)
        route_rows = jnp.where(mine, route_part, jnp.zeros((), BF16))
        route_rows = jnp.pad(route_rows, ((0, 0), (0, INFO - topk_count)))
        return jnp.concatenate([slot_back.astype(BF16), route_rows], 1)

    def weight_grads(recv_x, down_cot, dgate, dup, hidden):
        return [
            jnp.einsum("rd,rh->dh", a, b, preferred_element_type=F32)
            for a, b in ((recv_x, dgate), (recv_x, dup), (down_cot, hidden))
        ]

    away_slots, away_work = expert(away_recv, away_cot)
    away_back = rows_back(*away_slots)
    away_grads = lax.optimization_barrier(weight_grads(*away_work))
    near_cot, away_back = lax.optimization_barrier((near_cot, away_back))
    near_slots, near_work = expert(near_recv, near_cot)
    nx = lax.axis_size("x")
    xi = lax.axis_index("x")
    width = model_width // nx
    near_grads = weight_grads(*near_work)
    near_grads = [(a + b).astype(BF16) for a, b in zip(near_grads, away_grads)]
    owners = [jnp.where(xi + k >= nx, xi + k - nx, xi + k) for k in range(nx)]
    grad_local = jnp.stack(near_grads, 0)
    shares = [lax.dynamic_slice_in_dim(grad_local, owner * width, width, 1) for owner in owners]
    near_slots, shares = lax.optimization_barrier((near_slots, shares))
    near_back = rows_back(*near_slots)

    def combine(picks, rows):
        out = lax.dot_general(picks, rows, (((0,), (0,)), ((), ())), preferred_element_type=F32).astype(BF16)
        return [out[i * tok_count : (i + 1) * tok_count] for i in range(group)]

    def add(a, b):
        return (a.astype(F32) + b.astype(F32)).astype(BF16)

    away_ret = exchange(away_back)
    near_ret = exchange(near_back)
    part = {}
    part[2], part[-3], part[3], part[4] = combine(picks[1], away_ret)
    part[0], part[-1], part[1], part[-2] = combine(picks[0], near_ret)
    up = shift(part[4][:half], 1)
    down = shift(part[4][half:], -1)
    up = shift(jnp.concatenate([add(part[3][:half], up), part[3][half:]], 0), 1)
    down = shift(jnp.concatenate([part[-3][:half], add(part[-3][half:], down)], 0), -1)
    up_part, down_part = part[far - 2], part[2 - far]
    for k in range(far - 2, 0, -1):
        up_sum = add(up_part, up)
        up = shift(up_sum, 1)
        down_sum = add(down_part, down)
        down = shift(down_sum, -1)
        up_part, down_part, _, _ = lax.optimization_barrier((part[k - 1], part[1 - k], up_sum, down_sum))
    total = up_part.astype(F32) + up.astype(F32) + down.astype(F32)
    token_grad = total[:, :model_width].astype(BF16)
    routing_grad = total[:, model_width : model_width + topk_count].astype(BF16)

    for k in range(1, nx):
        shares[k] = lax.ppermute(shares[k], "x", [(i, (i + k) % nx) for i in range(nx)])
    grad_share = sum(g.astype(F32) for g in shares)[None]
    square = jnp.sum(grad_share * grad_share)
    square = jnp.broadcast_to(square, (1, INFO))
    square = square + lax.ppermute(square, "c", [(i, (i + 1) % nc) for i in range(nc)])
    square = jnp.broadcast_to(square[None], (nx * ny * nz, 1, INFO))
    square = lax.all_to_all(square, ("x", "y", "z"), split_axis=0, concat_axis=0, tiled=True)
    square_sum = jnp.sum(square[:, 0, 0])
    param_count = 3.0 * experts * model_width * hidden_units
    root_mean = jnp.sqrt(square_sum / param_count + 1e-06)
    clip_factor = jnp.minimum(1.0, 0.5 / root_mean)
    clipped = clip_factor * grad_share
    first_next = 0.9 * first_moment.astype(F32) + 0.1 * clipped
    second_next = 0.95 * second_moment.astype(F32) + 0.05 * clipped * clipped
    update = (
        first_next
        / (1.0 - 0.9**ADAM_STEP)
        / (jnp.sqrt(second_next / (1.0 - 0.95**ADAM_STEP)) + 1e-08)
    )
    return (
        token_grad,
        routing_grad,
        first_next.astype(BF16),
        second_next.astype(BF16),
        update.astype(BF16),
    )


def solution(mesh):
    tok = P(("x", "y", "z", "c"), None)
    ep = ("y", "z", "c")
    state = P(ep, None, "x", None)

    return jax.shard_map(
        on_device,
        mesh=plane(mesh),
        in_specs=(tok, tok, tok, tok, P(ep, None, None, None), state, state),
        out_specs=(tok, tok, state, state, state),
        check_vma=False,
    )
```
